32 devices in a mesh: tilt: 2 (over y), row: 4 (over z), col: 2 (over x), probe: 2 (over core).
Axes of the slice: x: 2, y: 2, z: 4, core: 2. Of those that a mesh axis runs over, the one named last changes fastest.
Arguments:
- object_tiles: bfloat16 [4, 2, 1536, 768], P('tilt', None, 'row', 'col'), parts along dimension 0, may hold values from -1 to 1
- probe_modes: bfloat16 [8, 4, 128, 128], P('probe', 'tilt'), parts along dimension 1, may hold values from -6 to 6
- amplitudes: bfloat16 [4, 2, 4, 128, 128], P('row', 'col', 'tilt'), parts along dimension 2, may hold values from 0 to 4
- positions: int32 [4, 2, 4, 2], P('row', 'col', 'tilt'), parts along dimension 2, may hold values from 0 to 448, as said below
- counts: int32 [8, 2], P(('tilt', 'row'), 'col'), parts along dimension 0, may hold values from 1 to 2, as said below
- tilt_shift: float32 [4], P('tilt'), parts along dimension 0, may hold values from -6 to 6
Outputs:
- updated: float32 [4, 2, 1536, 768], P('tilt', None, 'row', 'col'), parts along dimension 0
The draws below stay inside these ranges and needn't reach their ends.
There are 2 independent parts, one for each index of `tilt`. The reference program is written for one: setup_inputs(seed, part) draws one part's arguments, and reference() takes and returns one part's arrays. A program takes and returns all parts, laid end to end along the dimension named above; each array names one. Nothing has to cross between parts.
Inputs may be any that keep to these rules, and one draw needn't show every extreme that they name: Some tile has exactly 2 live positions; slots k >= counts of a tile are unused. `positions`: the extended frame's first pixel lies 96 pixels above and left of the tile's first core pixel.
All inputs are finite; a program needn't handle non-finite values.
Results may differ from the reference program's by a relative error of at most 0.0017.
Values may be sent and summed in bfloat16 or wider, within the bound.
No kernel may reach another device: no remote copies, remote signals or barrier semaphores. Data moves between devices by JAX's collectives and lax.ppermute only.
A program may use at most 64 MiB of HBM per device.

```python
import jax
import jax.numpy as jnp
from jax import lax

TILE = 384
MARGIN = 96
PSIDE = 128
SLICES = 2
NPOS_MAX = 2
MODES = 8
NR = 1536
NC = 768
EXT = 576
N_ROW = 4
N_COL = 2


def draw_counts(key, part):
    draw_one = jax.random.randint(jax.random.fold_in(key, 1), (N_ROW * N_COL,), 1, NPOS_MAX + 1)
    draw_two = jax.random.randint(jax.random.fold_in(key, 2), (N_ROW * N_COL,), 1, NPOS_MAX + 1)
    lowest = jnp.minimum(draw_one, draw_two)
    chosen = jax.random.randint(jax.random.fold_in(key, 3), (), 0, N_ROW * N_COL)
    filled = jnp.where(jnp.arange(N_ROW * N_COL) == chosen, NPOS_MAX, lowest)
    return filled.reshape(N_ROW, N_COL).astype(jnp.int32)


def draw_positions(key, part):
    offsets = jax.random.randint(jax.random.fold_in(key, 4), (N_ROW * N_COL, NPOS_MAX * 2), 0, EXT - PSIDE + 1)
    chosen = jax.random.randint(jax.random.fold_in(key, 5), (), 0, N_ROW * N_COL)
    tile_ids = jnp.arange(N_ROW * N_COL)[:, None]
    column_ids = jnp.arange(NPOS_MAX * 2)[None, :]
    offsets = jnp.where((tile_ids == chosen) & (column_ids < 2), EXT - PSIDE, offsets)
    offsets = jnp.where((tile_ids == (chosen + 1) % (N_ROW * N_COL)) & (column_ids < 2), 0, offsets)
    return offsets.reshape(N_ROW, N_COL, NPOS_MAX, 2).astype(jnp.int32)


def shard_levels(rng, extent, pieces, least, high):
    def one(axis_at, shards_of):
        draws = jax.random.uniform(jax.random.fold_in(jax.random.fold_in(rng, 6), axis_at), (shards_of,), jnp.float32, least / len(pieces), high / len(pieces))
        return jnp.repeat(jnp.exp(draws), extent[axis_at] // shards_of).reshape((-1,) + (1,) * (len(extent) - axis_at - 1))

    loudness = one(*pieces[0])
    for cut in pieces[1:]:
        loudness = loudness * one(*cut)
    return loudness


def gaussian(stream_key, dims, spread, reach, split=(), kind=jnp.bfloat16):
    entries = spread * jax.random.normal(stream_key, dims, jnp.float32)
    if split:
        entries = entries * shard_levels(stream_key, dims, split, -0.22, 0.18)
    return jnp.clip(entries, -reach, reach).astype(kind)


def setup_inputs(seed: int = 0, part: int = 0) -> dict:
    streams_of = jax.random.split(jax.random.key(seed), 7)
    part_splits = jax.random.split(jax.random.fold_in(streams_of[6], part), 7)
    object_tiles = jnp.clip(jax.random.uniform(part_splits[0], (SLICES, 2, NR, NC), jnp.float32, -1.0, 1.0) * shard_levels(part_splits[0], (SLICES, 2, NR, NC), ((2, 4), (3, 2)), -0.4, 0.0), -1.0, 1.0).astype(jnp.bfloat16)
    probe_modes = gaussian(part_splits[1], (MODES, 2, PSIDE, PSIDE), 1.0, 6.0, ((0, 2),))
    amplitudes = jnp.clip(4.0 * jax.random.uniform(part_splits[2], (N_ROW, N_COL, NPOS_MAX, PSIDE, PSIDE), jnp.float32) ** shard_levels(part_splits[2], (N_ROW, N_COL, NPOS_MAX, PSIDE, PSIDE), ((0, 4), (1, 2)), -0.2, 0.2), 0.0, 4.0).astype(jnp.bfloat16)
    positions = draw_positions(jax.random.fold_in(jax.random.fold_in(streams_of[6], part), 71), part)
    counts = draw_counts(jax.random.fold_in(jax.random.fold_in(streams_of[6], part), 71), part)
    tilt_shift = jnp.clip(jax.random.uniform(part_splits[5], (2,), jnp.float32, -6.0, 6.0), -6.0, 6.0)
    return dict(object_tiles=object_tiles, probe_modes=probe_modes, amplitudes=amplitudes, positions=positions, counts=counts, tilt_shift=tilt_shift)


FLOOR = 1.0
REGULAR = 1.0
CURVE = 1.5707963267948966
TWO_PI = 6.283185307179586

def kernel_table(probe_side, tilt_shift):
    grid_index = jnp.arange(probe_side, dtype=jnp.int32)
    centred = ((grid_index + probe_side // 2) % probe_side - probe_side // 2).astype(tilt_shift.dtype)
    chirp = CURVE * (centred[:, None] * centred[:, None] + centred[None, :] * centred[None, :]) / probe_side + TWO_PI * (tilt_shift[0] * centred[:, None] + tilt_shift[1] * centred[None, :]) / probe_side
    return lax.complex(jnp.cos(chirp), jnp.sin(chirp))

def power_of(field):
    return jnp.real(field) * jnp.real(field) + jnp.imag(field) * jnp.imag(field)

def reference(object_tiles, probe_modes, amplitudes, positions, counts, tilt_shift):
    start_object = object_tiles.astype(jnp.float32)
    padded = jnp.pad(start_object, ((0, 0), (0, 0), (MARGIN, MARGIN), (MARGIN, MARGIN)))
    probe_field = lax.complex(probe_modes[:, 0].astype(jnp.float32), probe_modes[:, 1].astype(jnp.float32))
    kernel = kernel_table(PSIDE, tilt_shift.astype(jnp.float32))
    probe_power = lax.optimization_barrier(jnp.sum(power_of(probe_field), axis=0))
    canvas = jnp.zeros((2, 3, NR + 2 * MARGIN, NC + 2 * MARGIN), jnp.float32)

    def tile_step(tile_index, canvas):
        tile_row = (tile_index // N_COL).astype(jnp.int32)
        tile_col = (tile_index % N_COL).astype(jnp.int32)
        live_count = counts[tile_row, tile_col]
        extended = lax.dynamic_slice(padded, (jnp.int32(0), jnp.int32(0), (tile_row * TILE).astype(jnp.int32), (tile_col * TILE).astype(jnp.int32)), (2, 2, EXT, EXT))

        def visit_slot(slot_index, gradient):
            corner = positions[tile_row, tile_col, slot_index].astype(jnp.int32)
            starts = (jnp.int32(0), jnp.int32(0), corner[0], corner[1])
            object_patch = lax.dynamic_slice(extended, starts, (2, 2, PSIDE, PSIDE))
            slice_one = lax.complex(object_patch[0, 0], object_patch[0, 1])
            slice_two = lax.complex(object_patch[1, 0], object_patch[1, 1])
            wave_field = jnp.fft.ifft2(kernel * jnp.fft.fft2(probe_field * slice_one, norm='ortho'), norm='ortho')
            far_field = jnp.fft.fft2(wave_field * slice_two, norm='ortho')
            modelled = jnp.sqrt(lax.optimization_barrier(jnp.sum(power_of(far_field), axis=0)))
            measured = amplitudes[tile_row, tile_col, slot_index].astype(jnp.float32)
            factor = 1.0 - measured / jnp.maximum(modelled, FLOOR)
            back_field = jnp.fft.ifft2(far_field * factor, norm='ortho')
            grad_two = lax.optimization_barrier(jnp.sum(jnp.conj(wave_field) * back_field, axis=0))
            light_two = lax.optimization_barrier(jnp.sum(power_of(wave_field), axis=0))
            entry_back = jnp.fft.ifft2(jnp.conj(kernel) * jnp.fft.fft2(jnp.conj(slice_two) * back_field, norm='ortho'), norm='ortho')
            grad_one = lax.optimization_barrier(jnp.sum(jnp.conj(probe_field) * entry_back, axis=0))
            update = jnp.stack([jnp.stack([jnp.real(grad_one), jnp.imag(grad_one), probe_power]), jnp.stack([jnp.real(grad_two), jnp.imag(grad_two), light_two])])
            weight = (slot_index < live_count).astype(update.dtype)
            current = lax.dynamic_slice(gradient, starts, (2, 3, PSIDE, PSIDE))
            return lax.dynamic_update_slice(gradient, current + weight * update, starts)
        gradient = lax.fori_loop(0, NPOS_MAX, visit_slot, jnp.zeros((2, 3, EXT, EXT), jnp.float32))
        anchor = (jnp.int32(0), jnp.int32(0), (tile_row * TILE).astype(jnp.int32), (tile_col * TILE).astype(jnp.int32))
        region = lax.dynamic_slice(canvas, anchor, (2, 3, EXT, EXT))
        return lax.dynamic_update_slice(canvas, region + gradient, anchor)
    canvas = lax.fori_loop(0, N_ROW * N_COL, tile_step, canvas)
    summed = canvas[:, :, MARGIN:MARGIN + NR, MARGIN:MARGIN + NC]
    return start_object - summed[:, 0:2] / (summed[:, 2:3] + REGULAR)
```

```python
import functools

import jax
import jax.numpy as jnp
import numpy as np
from jax import lax
from jax.experimental import pallas as pl
from jax.experimental.pallas import tpu as pltpu
from jax.sharding import PartitionSpec as P

MARGIN = 96
FLOOR = 1.0
REGULAR = 1.0
LANES = 128
TAIL = 16
BF = jnp.bfloat16
F32 = jnp.float32
VMEM = pl.BlockSpec(memory_space=pltpu.VMEM)
SMEM = pl.BlockSpec(memory_space=pltpu.SMEM)


def partner(index, phase, size):
    other = (index ^ 1) if phase == 0 else ((index + 1) ^ 1) - 1
    return other if 0 <= other < size else None


def phases_of(size):
    return [ph for ph in (0, 1) if any(partner(i, ph, size) is not None for i in range(size))]


def swap_pairs(sizes, row_phase, col_phase):
    rows, cols, cores = sizes
    pairs = []
    for r in range(rows):
        for c in range(cols):
            r2 = r if row_phase is None else partner(r, row_phase, rows)
            c2 = c if col_phase is None else partner(c, col_phase, cols)
            if r2 is None or c2 is None:
                continue
            for k in range(cores):
                pairs.append(((r * cols + c) * cores + k, (r2 * cols + c2) * cores + k))
    return pairs


def is_after(axis, phase):
    index = lax.axis_index(axis)
    return jnp.where(lax.rem(index, 2) == phase, 1, 0).astype(jnp.int32)


def onehot(shape, fn):
    i = lax.broadcasted_iota(jnp.int32, shape, 0)
    j = lax.broadcasted_iota(jnp.int32, shape, 1)
    return jnp.where(fn(i, j), 1.0, 0.0).astype(BF)


def dot(a, b):
    return jnp.dot(a, b, preferred_element_type=F32)


def split(x):
    hi = x.astype(BF)
    return hi, (x - hi.astype(F32)).astype(BF)


def prep_kernel(plan, obj_ref, *outs):
    planes, side, _ = obj_ref.shape
    m = MARGIN
    edge = -(-m // LANES) * LANES
    z_refs, x_refs, d_refs = outs[: len(plan.rows)], outs[len(plan.rows) : len(plan.rows) + len(plan.cols)], outs[len(plan.rows) + len(plan.cols) :]
    starts = [pl.multiple_of(is_after("row", ph) * (side - m), 32) for ph in plan.rows]
    for z_ref, start in zip(z_refs, starts):
        for p in range(planes):
            z_ref[p * m : (p + 1) * m, :] = obj_ref[p, pl.ds(start, m), :]
    d_iter = iter(d_refs)
    for x_ref, pc in zip(x_refs, plan.cols):
        after = is_after("col", pc)
        lane0 = pl.multiple_of(after * (side - edge), LANES)
        offset = after * (edge - m)
        stack = jnp.concatenate([obj_ref[p, :, pl.ds(lane0, edge)] for p in range(planes)], axis=1)

        def pick(i, j):
            local, lane = i % edge - offset, j % m
            return (i // edge == j // m) & (local == lane)

        x_ref[...] = dot(stack, onehot((planes * edge, planes * m), pick)).astype(BF)
    for ph_start in starts:
        for x_ref in x_refs:
            next(d_iter)[...] = x_ref[pl.ds(ph_start, m), :]


def right_pack(re, im):
    return jnp.concatenate([jnp.concatenate([re, im], 1), jnp.concatenate([-im, re], 1)], 0)


def left_pack(re, im):
    return jnp.concatenate([jnp.concatenate([re, -im], 1), jnp.concatenate([im, re], 1)], 0)


def table_kernel(f_ref, h_ref, out_ref):
    n = f_ref.shape[1]
    fr, fi = f_ref[0], f_ref[1]

    def circulant(hr, hi):
        vr, vi = fr * hr + fi * hi, fr * hi - fi * hr
        a_hi, a_lo = split(left_pack(vr, vi))
        b_hi, b_lo = split(left_pack(fr, fi))
        return dot(a_hi, b_hi) + (dot(a_lo, b_hi) + dot(a_hi, b_lo)) + dot(a_lo, b_lo)

    def store(at, value):
        hi, lo = split(value)
        out_ref[2 * at] = hi
        out_ref[2 * at + 1] = lo

    h0r, h0i, h1r, h1i = (h_ref[k : k + 1, :] for k in range(4))
    left = circulant(h0r, h0i)
    left_adj = circulant(h0r, -h0i)
    across = circulant(h1r, h1i)
    rt = across[:n, :n].T
    it = across[n:, :n].T
    store(0, left)
    store(1, right_pack(rt, it))
    store(2, left_adj)
    store(3, right_pack(across[:n, :n], -across[n:, :n]))


def main_kernel(plan, *refs):
    refs = list(refs)
    pos_ref, cnt_ref, obj_ref = refs[:3]
    refs = refs[3:]
    n_row, n_col = len(plan.rows), len(plan.cols)
    z_in, refs = refs[:n_row], refs[n_row:]
    x_in, refs = refs[:n_col], refs[n_col:]
    d_in, refs = refs[: n_row * n_col], refs[n_row * n_col :]
    q_refs, refs = refs[: plan.cores], refs[plan.cores :]
    amp_ref, fpack_ref, prop_ref = refs[:3]
    refs = refs[3:]
    z_out, refs = refs[:n_row], refs[n_row:]
    x_out, refs = refs[:n_col], refs[n_col:]
    d_out, refs = refs[: n_row * n_col], refs[n_row * n_col :]
    g_out, wave_ref, far_ref, gsum_ref = refs

    planes, side, _ = obj_ref.shape
    n = amp_ref.shape[1]
    m = MARGIN
    slot = lax.axis_index("probe")
    a, b = pos_ref[slot, 0], pos_ref[slot, 1]
    live = slot < cnt_ref[0, 0]

    row0 = [is_after("row", ph) * (side + m) for ph in plan.rows]
    col0 = [is_after("col", ph) * (side + m) for ph in plan.cols]

    r_own = onehot((n, side), lambda i, j: j + m == a + i)
    r_strip = [onehot((n, m), lambda i, j, o=o: j + o == a + i) for o in row0]
    c_own = onehot((side, n), lambda i, j: i + m == b + j)

    def rows_of(own, strips):
        value = dot(r_own, own)
        for r, s in zip(r_strip, strips):
            value += dot(r, s)
        return value.astype(BF)

    packed = [
        rows_of(x_in[c][...], [d_in[ph * n_col + c][...] for ph in range(n_row)]) for c in range(n_col)
    ]
    window = []
    for p in range(planes):
        cut = rows_of(obj_ref[p], [z[p * m : (p + 1) * m, :] for z in z_in])
        value = dot(cut, c_own)
        for c in range(n_col):
            pick = onehot(
                (planes * m, n),
                lambda i, j, o=col0[c], p=p: (i >= p * m) & (i < (p + 1) * m) & (i - p * m + o == b + j),
            )
            value += dot(packed[c], pick)
        window.append(value)
    p1r, p1i, p2r, p2i = window

    f_hi, f_lo, fc_hi, fc_lo = (fpack_ref[k] for k in range(4))

    def rmul(x, t_hi, t_lo):
        hi, lo = split(x)
        return dot(hi, t_hi) + (dot(lo, t_hi) + dot(hi, t_lo))

    def lmul(t_hi, t_lo, x):
        hi, lo = split(x)
        return dot(t_hi, hi) + (dot(t_hi, lo) + dot(t_lo, hi))

    def two_sided(parts, left, right):
        x = jnp.concatenate([jnp.concatenate(p, 1) for p in parts], 0)
        y = rmul(x, *right)
        k = len(parts)
        z = jnp.concatenate(
            [
                jnp.concatenate([y[i * n : (i + 1) * n, :n] for i in range(k)], 1),
                jnp.concatenate([y[i * n : (i + 1) * n, n:] for i in range(k)], 1),
            ],
            0,
        )
        w = lmul(*left, z)
        return [(w[:n, i * n : (i + 1) * n], w[n:, i * n : (i + 1) * n]) for i in range(k)]

    dft = dict(left=(fc_hi, fc_lo), right=(f_hi, f_lo))
    inv = dict(left=(f_hi, f_lo), right=(fc_hi, fc_lo))
    prop = dict(left=(prop_ref[0], prop_ref[1]), right=(prop_ref[2], prop_ref[3]))
    adj = dict(left=(prop_ref[4], prop_ref[5]), right=(prop_ref[6], prop_ref[7]))

    local = q_refs[0].shape[0]
    order = [(c, k) for c in range(plan.cores) for k in range(local)]
    pairs = [order[i : i + 2] for i in range(0, len(order), 2)]

    def probe(c, k):
        return q_refs[c][k, 0].astype(F32), q_refs[c][k, 1].astype(F32)

    power = jnp.zeros((n, n), F32)
    at = 0
    for pair in pairs:
        parts = []
        for c, k in pair:
            qr, qi = probe(c, k)
            parts.append((qr * p1r - qi * p1i, qr * p1i + qi * p1r))
        waves = two_sided(parts, **prop)
        parts = []
        for i, (wr, wi) in enumerate(waves):
            wave_ref[at + i, 0] = wr
            wave_ref[at + i, 1] = wi
            parts.append((wr * p2r - wi * p2i, wr * p2i + wi * p2r))
        fars = two_sided(parts, **dft)
        for i, (fr, fi) in enumerate(fars):
            far_ref[at + i, 0] = fr
            far_ref[at + i, 1] = fi
            power += fr * fr + fi * fi
        at += len(pair)

    factor = 1.0 - amp_ref[slot].astype(F32) / jnp.maximum(jnp.sqrt(power), FLOOR)
    at = 0
    gsum_ref[...] = jnp.zeros_like(gsum_ref)
    for pair in pairs:
        parts = [(far_ref[at + i, 0] * factor, far_ref[at + i, 1] * factor) for i in range(len(pair))]
        backs = two_sided(parts, **inv)
        parts = []
        for i, (br, bi) in enumerate(backs):
            wr, wi = wave_ref[at + i, 0], wave_ref[at + i, 1]
            gsum_ref[3] += wr * br + wi * bi
            gsum_ref[4] += wr * bi - wi * br
            gsum_ref[5] += wr * wr + wi * wi
            parts.append((p2r * br + p2i * bi, p2r * bi - p2i * br))
        entries = two_sided(parts, **adj)
        for (er, ei), (c, k) in zip(entries, pair):
            qr, qi = probe(c, k)
            gsum_ref[0] += qr * er + qi * ei
            gsum_ref[1] += qr * ei - qi * er
            gsum_ref[2] += qr * qr + qi * qi
        at += len(pair)

    grads = gsum_ref.shape[0]
    for p in range(grads):
        g_out[p * n : (p + 1) * n, :] = jnp.where(live, gsum_ref[p], 0.0).astype(BF)

    def digits(shape, value):
        i = lax.broadcasted_iota(jnp.int32, shape, 0)
        high = lax.shift_right_logical(value, 4)
        low = value & 15
        return jnp.where(i == 0, high, jnp.where(i == 1, low, 0)).astype(F32).astype(BF)

    r_out = [onehot((m, n), lambda i, j, o=o: i + o == a + j) for o in row0]
    for z, r in zip(z_out, r_out):
        for p in range(grads):
            z[p * m : (p + 1) * m, :] = dot(r, g_out[p * n : (p + 1) * n, :]).astype(BF)
        z[grads * m :, :] = digits((TAIL, n), b)
    for c, x in enumerate(x_out):
        value = jnp.zeros((n, grads * m), F32)
        for p in range(grads):
            pick = onehot(
                (n, grads * m),
                lambda i, j, o=col0[c], p=p: (j >= p * m) & (j < (p + 1) * m) & (j - p * m + o == b + i),
            )
            value += dot(g_out[p * n : (p + 1) * n, :], pick)
        x[:n, :] = value.astype(BF)
        x[n:, :] = digits((TAIL, grads * m), a)
        for ph, r in enumerate(r_out):
            d_out[ph * n_col + c][...] = dot(r, x[:n, :]).astype(BF)


def final_kernel(plan, *refs):
    refs = list(refs)
    pos_ref, obj_ref = refs[:2]
    refs = refs[2:]
    n_row, n_col, cores = len(plan.rows), len(plan.cols), plan.cores

    def take(k):
        nonlocal refs
        head, refs = refs[:k], refs[k:]
        return head

    g_in = take(cores)
    z_in = [take(cores) for _ in range(n_row)]
    x_in = [take(cores) for _ in range(n_col)]
    d_in = [take(cores) for _ in range(n_row * n_col)]
    out_ref, u_ref, acc_ref = refs

    planes, block, side = obj_ref.shape
    n = g_in[0].shape[1]
    m = MARGIN
    grads = g_in[0].shape[0] // n
    step = pl.program_id(0)
    last = pl.num_programs(0) - 1
    me = lax.axis_index("probe")
    slots = [lax.rem(me + j, cores) for j in range(cores)]
    edge = -(-m // LANES) * LANES

    @pl.when(step == 0)
    def _():
        for j, g in enumerate(g_in):
            b = pos_ref[slots[j], 1]
            spread = onehot((n, side), lambda i, l: l + m == b + i)
            wide = dot(g[...], spread).astype(BF)
            for p in range(grads):
                u_ref[p, j * n : (j + 1) * n, :] = wide[p * n : (p + 1) * n, :]

    top = step * block + m
    rows = jnp.concatenate(
        [onehot((block, n), lambda i, w, j=j: i + top == pos_ref[slots[j], 0] + w) for j in range(cores)], 1
    )
    for p in range(grads):
        acc_ref[p] = dot(rows, u_ref[p])

    def decode(value):
        return (value[0:1, :].astype(F32) * 16.0 + value[1:2, :].astype(F32)).astype(jnp.int32)

    touched = []
    for ph in range(n_row):
        after = is_after("row", plan.rows[ph])
        touched.append(step == after * last)

        @pl.when(touched[ph])
        def _(ph=ph):
            spreads = []
            for z in z_in[ph]:
                b = decode(z[grads * m :, :])
                i = lax.broadcasted_iota(jnp.int32, (side, n), 0)
                w = lax.broadcasted_iota(jnp.int32, (side, n), 1)
                spreads.append(jnp.where(i + m == b + w, 1.0, 0.0).astype(BF))
            for p in range(grads):
                value = None
                for z, s in zip(z_in[ph], spreads):
                    term = lax.dot_general(
                        z[p * m : (p + 1) * m, :], s, (((1,), (1,)), ((), ())), preferred_element_type=F32
                    )
                    value = term if value is None else value + term
                acc_ref[p] += value

    for c in range(n_col):
        after = is_after("col", plan.cols[c])
        value = None
        for x in x_in[c]:
            a = decode(x[n:, :LANES])
            w = lax.broadcasted_iota(jnp.int32, (n, block), 0)
            i = lax.broadcasted_iota(jnp.int32, (n, block), 1)
            place = jnp.where(i + top == a[:, :block] + w, 1.0, 0.0).astype(BF)
            term = lax.dot_general(
                place, x[:n, :], (((0,), (0,)), ((), ())), preferred_element_type=F32
            )
            value = term if value is None else value + term
        for ph in range(n_row):
            both = None
            for d in d_in[ph * n_col + c]:
                term = d[...].astype(F32)
                both = term if both is None else both + term
            value += jnp.where(touched[ph], both, 0.0)
        hi, lo = split(value)
        lane0 = pl.multiple_of(after * (side - edge), LANES)
        offset = after * (edge - m)
        for p in range(grads):
            pick = onehot(
                (grads * m, edge),
                lambda i, l, p=p: (i >= p * m) & (i < (p + 1) * m) & (i - p * m + offset == l),
            )
            acc_ref[p, :, pl.ds(lane0, edge)] += dot(hi, pick) + dot(lo, pick)

    per = 3
    for s in range(grads // per):
        light = acc_ref[per * s + 2] + REGULAR
        for k in range(2):
            out_ref[2 * s + k] = obj_ref[2 * s + k].astype(F32) - acc_ref[per * s + k] / light


class Plan:
    def __init__(self, mesh):
        self.sizes = (mesh.shape["row"], mesh.shape["col"], mesh.shape["probe"])
        self.rows = phases_of(self.sizes[0])
        self.cols = phases_of(self.sizes[1])
        self.cores = self.sizes[2]

    def swap(self, value, row_phase, col_phase):
        return lax.ppermute(value, ("row", "col", "probe"), swap_pairs(self.sizes, row_phase, col_phase))

    def others(self, value):
        n = self.cores
        return [value] + [lax.ppermute(value, "probe", [((i + j) % n, i) for i in range(n)]) for j in range(1, n)]


def dft_pack(n):
    k = np.arange(n)
    phase = 2.0 * np.pi * ((k[:, None] * k[None, :]) % n) / n
    fr, fi = np.cos(phase) / np.sqrt(n), -np.sin(phase) / np.sqrt(n)
    return fr.astype(np.float32), fi.astype(np.float32)


def chirps(n, tilt_shift):
    u = jnp.arange(n, dtype=jnp.int32)
    u = (u + n // 2) % n - n // 2
    curve = ((u * u) % (4 * n)).astype(F32) / (4 * n)
    turns = tilt_shift[:, None] * u.astype(F32)[None, :] / n
    phase = (2.0 * np.pi) * (curve[None, :] + (turns - jnp.round(turns)))
    return jnp.stack([jnp.cos(phase), jnp.sin(phase)], 1).reshape(-1, n)


def body(plan, object_tiles, probe_modes, amplitudes, positions, counts, tilt_shift):
    slices, _, side, _ = object_tiles.shape
    planes = slices * 2
    n = probe_modes.shape[2]
    m = MARGIN
    grads = slices * 3
    slot_total = amplitudes.shape[2]
    assert slot_total == plan.cores
    obj = object_tiles.reshape(planes, side, side)
    pos = positions[0, 0]
    n_row, n_col = len(plan.rows), len(plan.cols)
    combos = [(r, c) for r in plan.rows for c in plan.cols]

    def sds(shape, dtype=BF):
        return jax.ShapeDtypeStruct(shape, dtype)

    strips = pl.pallas_call(
        functools.partial(prep_kernel, plan),
        out_shape=[sds((planes * m, side))] * n_row
        + [sds((side, planes * m))] * n_col
        + [sds((m, planes * m))] * len(combos),
        in_specs=[VMEM],
        out_specs=[VMEM] * (n_row + n_col + len(combos)),
        name="strips",
    )(obj)
    links = [(r, None) for r in plan.rows] + [(None, c) for c in plan.cols] + combos
    arrived = [plan.swap(v, *link) for v, link in zip(strips, links)]

    modes = plan.others(probe_modes)
    fr, fi = dft_pack(n)

    def np_split(x):
        hi = x.astype(jnp.bfloat16)
        return hi, (x - hi.astype(np.float32)).astype(jnp.bfloat16)

    fpack = np.block([[fr, fi], [-fi, fr]])
    fcpack = np.block([[fr, -fi], [fi, fr]])
    fpacks = jnp.asarray(np.stack([*np_split(fpack), *np_split(fcpack)]))
    props = pl.pallas_call(
        table_kernel,
        out_shape=sds((8, 2 * n, 2 * n)),
        in_specs=[VMEM, VMEM],
        out_specs=VMEM,
        name="tables",
        cost_estimate=pl.CostEstimate(flops=10**9, bytes_accessed=10**6, transcendentals=0),
    )(jnp.asarray(np.stack([fr, fi])), chirps(n, tilt_shift))

    modes_total = plan.cores * probe_modes.shape[0]
    msgs = pl.pallas_call(
        functools.partial(main_kernel, plan),
        out_shape=[sds((grads * m + TAIL, n))] * n_row
        + [sds((n + TAIL, grads * m))] * n_col
        + [sds((m, grads * m))] * len(combos)
        + [sds((grads * n, n))],
        in_specs=[SMEM, SMEM] + [VMEM] * (1 + len(links) + plan.cores + 3),
        out_specs=[VMEM] * (len(links) + 1),
        scratch_shapes=[
            pltpu.VMEM((modes_total, 2, n, n), F32),
            pltpu.VMEM((modes_total, 2, n, n), F32),
            pltpu.VMEM((grads, n, n), F32),
        ],
        name="waves",
    )(pos, counts, obj, *arrived, *modes, amplitudes[0, 0], fpacks, props)
    own = plan.others(msgs[-1])
    pieces = [plan.others(plan.swap(v, *link)) for v, link in zip(msgs[:-1], links)]
    flat = list(own) + [v for group in pieces for v in group]

    block = m
    const = lambda v: pl.BlockSpec(v.shape, lambda i: (0,) * v.ndim)
    updated = pl.pallas_call(
        functools.partial(final_kernel, plan),
        grid=(side // block,),
        out_shape=sds((planes, side, side), F32),
        in_specs=[SMEM, pl.BlockSpec((planes, block, side), lambda i: (0, i, 0))] + [const(v) for v in flat],
        out_specs=pl.BlockSpec((planes, block, side), lambda i: (0, i, 0)),
        scratch_shapes=[
            pltpu.VMEM((grads, plan.cores * n, side), BF),
            pltpu.VMEM((grads, block, side), F32),
        ],
        name="fold",
    )(pos, obj, *flat)
    return updated.reshape(object_tiles.shape)


def solution(mesh):
    plan = Plan(mesh)
    return jax.shard_map(
        functools.partial(body, plan),
        mesh=mesh,
        in_specs=(
            P("tilt", None, "row", "col"),
            P("probe", "tilt", None, None),
            P("row", "col", "tilt", None, None),
            P("row", "col", "tilt", None),
            P(("tilt", "row"), "col"),
            P("tilt"),
        ),
        out_specs=P("tilt", None, "row", "col"),
        check_vma=False,
    )
```

```python
import functools

import jax
import jax.numpy as jnp
import numpy as np
from jax import lax
from jax.experimental import pallas as pl
from jax.experimental.pallas import tpu as pltpu
from jax.sharding import PartitionSpec as P

MARGIN = 96
FLOOR = 1.0
REGULAR = 1.0
LANES = 128
TAIL = 16
GROUP = 2
BF = jnp.bfloat16
F32 = jnp.float32
VMEM = pl.BlockSpec(memory_space=pltpu.VMEM)
SMEM = pl.BlockSpec(memory_space=pltpu.SMEM)


def partner(index, phase, size):
    other = (index ^ 1) if phase == 0 else ((index + 1) ^ 1) - 1
    return other if 0 <= other < size else None


def phases_of(size):
    return [ph for ph in (0, 1) if any(partner(i, ph, size) is not None for i in range(size))]


def swap_pairs(sizes, row_phase, col_phase):
    rows, cols, cores = sizes
    pairs = []
    for r in range(rows):
        for c in range(cols):
            r2 = r if row_phase is None else partner(r, row_phase, rows)
            c2 = c if col_phase is None else partner(c, col_phase, cols)
            if r2 is None or c2 is None:
                continue
            for k in range(cores):
                pairs.append(((r * cols + c) * cores + k, (r2 * cols + c2) * cores + k))
    return pairs


def is_after(axis, phase):
    index = lax.axis_index(axis)
    return jnp.where(lax.rem(index, 2) == phase, 1, 0).astype(jnp.int32)


def onehot(shape, fn):
    i = lax.broadcasted_iota(jnp.int32, shape, 0)
    j = lax.broadcasted_iota(jnp.int32, shape, 1)
    return jnp.where(fn(i, j), 1.0, 0.0).astype(BF)


def dot(a, b):
    return jnp.dot(a, b, preferred_element_type=F32)


def split(x):
    hi = x.astype(BF)
    return hi, (x - hi.astype(F32)).astype(BF)


def prep_kernel(plan, obj_ref, *outs):
    planes, side, _ = obj_ref.shape
    m = MARGIN
    edge = -(-m // LANES) * LANES
    z_refs, x_refs, d_refs = outs[: len(plan.rows)], outs[len(plan.rows) : len(plan.rows) + len(plan.cols)], outs[len(plan.rows) + len(plan.cols) :]
    starts = [pl.multiple_of(is_after("row", ph) * (side - m), 32) for ph in plan.rows]
    for z_ref, start in zip(z_refs, starts):
        for p in range(planes):
            z_ref[p * m : (p + 1) * m, :] = obj_ref[p, pl.ds(start, m), :]
    d_iter = iter(d_refs)
    for x_ref, pc in zip(x_refs, plan.cols):
        after = is_after("col", pc)
        lane0 = pl.multiple_of(after * (side - edge), LANES)
        offset = after * (edge - m)
        stack = jnp.concatenate([obj_ref[p, :, pl.ds(lane0, edge)] for p in range(planes)], axis=1)

        def pick(i, j):
            local, lane = i % edge - offset, j % m
            return (i // edge == j // m) & (local == lane)

        x_ref[...] = dot(stack, onehot((planes * edge, planes * m), pick)).astype(BF)
    for ph_start in starts:
        for x_ref in x_refs:
            next(d_iter)[...] = x_ref[pl.ds(ph_start, m), :]


def right_pack(re, im):
    return jnp.concatenate([jnp.concatenate([re, im], 1), jnp.concatenate([-im, re], 1)], 0)


def left_pack(re, im):
    return jnp.concatenate([jnp.concatenate([re, -im], 1), jnp.concatenate([im, re], 1)], 0)


def table_kernel(f_ref, h_ref, out_ref):
    n = f_ref.shape[1]
    fr, fi = f_ref[0], f_ref[1]

    def circulant(hr, hi):
        vr, vi = fr * hr + fi * hi, fr * hi - fi * hr
        a_hi, a_lo = split(left_pack(vr, vi))
        b_hi, b_lo = split(left_pack(fr, fi))
        return dot(a_hi, b_hi) + (dot(a_lo, b_hi) + dot(a_hi, b_lo)) + dot(a_lo, b_lo)

    def store(at, value):
        hi, lo = split(value)
        out_ref[2 * at] = hi
        out_ref[2 * at + 1] = lo

    for axis in (0, 1):
        table = circulant(h_ref[2 * axis : 2 * axis + 1, :], h_ref[2 * axis + 1 : 2 * axis + 2, :])
        store(2 * axis, table.T)
        store(2 * axis + 1, table)


def main_kernel(plan, *refs):
    refs = list(refs)
    pos_ref, cnt_ref, obj_ref = refs[:3]
    refs = refs[3:]
    n_row, n_col = len(plan.rows), len(plan.cols)
    z_in, refs = refs[:n_row], refs[n_row:]
    x_in, refs = refs[:n_col], refs[n_col:]
    d_in, refs = refs[: n_row * n_col], refs[n_row * n_col :]
    q_refs, refs = refs[: plan.cores], refs[plan.cores :]
    amp_ref, fpack_ref, prop_ref = refs[:3]
    refs = refs[3:]
    z_out, refs = refs[:n_row], refs[n_row:]
    x_out, refs = refs[:n_col], refs[n_col:]
    d_out, refs = refs[: n_row * n_col], refs[n_row * n_col :]
    g_out, wave_ref, far_ref, gsum_ref, hi_ref, lo_ref = refs

    planes, side, _ = obj_ref.shape
    n = amp_ref.shape[1]
    m = MARGIN
    slot = lax.axis_index("probe")
    a, b = pos_ref[slot, 0], pos_ref[slot, 1]
    live = slot < cnt_ref[0, 0]

    row0 = [is_after("row", ph) * (side + m) for ph in plan.rows]
    col0 = [is_after("col", ph) * (side + m) for ph in plan.cols]

    r_own = onehot((n, side), lambda i, j: j + m == a + i)
    r_strip = [onehot((n, m), lambda i, j, o=o: j + o == a + i) for o in row0]
    c_own = onehot((side, n), lambda i, j: i + m == b + j)

    def rows_of(own, strips):
        value = dot(r_own, own)
        for r, s in zip(r_strip, strips):
            value += dot(r, s)
        return value.astype(BF)

    packed = [
        rows_of(x_in[c][...], [d_in[ph * n_col + c][...] for ph in range(n_row)]) for c in range(n_col)
    ]
    window = []
    for p in range(planes):
        cut = rows_of(obj_ref[p], [z[p * m : (p + 1) * m, :] for z in z_in])
        value = dot(cut, c_own)
        for c in range(n_col):
            pick = onehot(
                (planes * m, n),
                lambda i, j, o=col0[c], p=p: (i >= p * m) & (i < (p + 1) * m) & (i - p * m + o == b + j),
            )
            value += dot(packed[c], pick)
        window.append(value)
    p1r, p1i, p2r, p2i = window

    p2r, p2i = p2r.T, p2i.T

    dft = (fpack_ref[0], fpack_ref[1])
    inv = (fpack_ref[2], fpack_ref[3])
    fwd_rows, adj_rows, fwd_cols, adj_cols = ((prop_ref[2 * k], prop_ref[2 * k + 1]) for k in range(4))

    local = q_refs[0].shape[0]
    modes = local * plan.cores
    group = min(GROUP, modes)

    def probe(mode):
        q = q_refs[mode // local]
        return q[mode % local, 0].astype(F32), q[mode % local, 1].astype(F32)

    def put(side, mode, re, im):
        rows = slice(mode * n, (mode + 1) * n)
        for part, value in enumerate((re, im)):
            hi, lo = split(value)
            lanes = slice(part * n, (part + 1) * n)
            hi_ref[side, rows, lanes] = hi
            lo_ref[side, rows, lanes] = lo

    queue = []

    def product(side, table, finish):
        t_hi, t_lo = table
        for first in range(0, modes, group):
            rows = slice(first * n, (first + group) * n)
            hi, lo = hi_ref[side, rows, :], lo_ref[side, rows, :]
            y = dot(hi, t_hi) + dot(lo, t_hi) + dot(hi, t_lo)
            parts = [(y[i * n : (i + 1) * n, :n], y[i * n : (i + 1) * n, n:]) for i in range(group)]
            queue.append(functools.partial(finish, first, parts))
            if len(queue) > 1:
                queue.pop(0)()

    def drain():
        while queue:
            queue.pop(0)()

    def turned(side):
        def finish(first, parts):
            for i, (re, im) in enumerate(parts):
                put(side, first + i, re.T, im.T)

        return finish

    for mode in range(modes):
        qr, qi = probe(mode)
        put(0, mode, qr * p1r - qi * p1i, qr * p1i + qi * p1r)

    def at_slice_2(first, parts):
        for i, (wr, wi) in enumerate(parts):
            wave_ref[first + i, 0] = wr
            wave_ref[first + i, 1] = wi
            put(0, first + i, wr * p2r - wi * p2i, wr * p2i + wi * p2r)

    def at_detector(first, parts):
        total = sum(fr * fr + fi * fi for fr, fi in parts)
        gsum_ref[0] = total if first == 0 else gsum_ref[0] + total
        for i, (fr, fi) in enumerate(parts):
            far_ref[first + i, 0] = fr
            far_ref[first + i, 1] = fi

    product(0, fwd_cols, turned(1))
    product(1, fwd_rows, at_slice_2)
    product(0, dft, turned(1))
    product(1, dft, at_detector)
    drain()

    factor = 1.0 - amp_ref[slot].astype(F32) / jnp.maximum(jnp.sqrt(gsum_ref[0]), FLOOR)
    for mode in range(modes):
        put(0, mode, far_ref[mode, 0] * factor, far_ref[mode, 1] * factor)

    def back_at_slice_2(first, parts):
        sums = [0.0, 0.0, 0.0]
        for i, (br, bi) in enumerate(parts):
            wr, wi = wave_ref[first + i, 0], wave_ref[first + i, 1]
            sums[0] += wr * br + wi * bi
            sums[1] += wr * bi - wi * br
            sums[2] += wr * wr + wi * wi
            put(0, first + i, p2r * br + p2i * bi, p2r * bi - p2i * br)
        for k, value in enumerate(sums):
            gsum_ref[3 + k] = value if first == 0 else gsum_ref[3 + k] + value

    def back_at_slice_1(first, parts):
        sums = [0.0, 0.0, 0.0]
        for i, (er, ei) in enumerate(parts):
            qr, qi = probe(first + i)
            sums[0] += qr * er + qi * ei
            sums[1] += qr * ei - qi * er
            sums[2] += qr * qr + qi * qi
        for k, value in enumerate(sums):
            gsum_ref[k] = value if first == 0 else gsum_ref[k] + value

    product(0, inv, turned(1))
    product(1, inv, back_at_slice_2)
    product(0, adj_rows, turned(1))
    product(1, adj_cols, back_at_slice_1)
    drain()
    for k in range(3, 6):
        gsum_ref[k] = gsum_ref[k].T

    grads = gsum_ref.shape[0]
    for p in range(grads):
        g_out[p * n : (p + 1) * n, :] = jnp.where(live, gsum_ref[p], 0.0).astype(BF)

    def digits(shape, value):
        i = lax.broadcasted_iota(jnp.int32, shape, 0)
        high = lax.shift_right_logical(value, 4)
        low = value & 15
        return jnp.where(i == 0, high, jnp.where(i == 1, low, 0)).astype(F32).astype(BF)

    r_out = [onehot((m, n), lambda i, j, o=o: i + o == a + j) for o in row0]
    for z, r in zip(z_out, r_out):
        for p in range(grads):
            z[p * m : (p + 1) * m, :] = dot(r, g_out[p * n : (p + 1) * n, :]).astype(BF)
        z[grads * m :, :] = digits((TAIL, n), b)
    for c, x in enumerate(x_out):
        value = jnp.zeros((n, grads * m), F32)
        for p in range(grads):
            pick = onehot(
                (n, grads * m),
                lambda i, j, o=col0[c], p=p: (j >= p * m) & (j < (p + 1) * m) & (j - p * m + o == b + i),
            )
            value += dot(g_out[p * n : (p + 1) * n, :], pick)
        x[:n, :] = value.astype(BF)
        x[n:, :] = digits((TAIL, grads * m), a)
        for ph, r in enumerate(r_out):
            d_out[ph * n_col + c][...] = dot(r, x[:n, :]).astype(BF)


def final_kernel(plan, *refs):
    refs = list(refs)
    pos_ref, obj_ref = refs[:2]
    refs = refs[2:]
    n_row, n_col, cores = len(plan.rows), len(plan.cols), plan.cores

    def take(k):
        nonlocal refs
        head, refs = refs[:k], refs[k:]
        return head

    g_in = take(cores)
    z_in = [take(cores) for _ in range(n_row)]
    x_in = [take(cores) for _ in range(n_col)]
    d_in = [take(cores) for _ in range(n_row * n_col)]
    out_hbm, acc_ref, out_ref, sem = refs

    planes, side, _ = obj_ref.shape
    n = g_in[0].shape[1]
    m = MARGIN
    grads = g_in[0].shape[0] // n
    me = lax.axis_index("probe")
    edge = -(-m // LANES) * LANES
    tall, broad = n + TAIL, min(n + LANES, side)

    def decode(value):
        return (value[0:1, :].astype(F32) * 16.0 + value[1:2, :].astype(F32)).astype(jnp.int32)

    def same(left, right):
        return jnp.where(left == right, 1.0, 0.0).astype(BF)

    def grid2(shape):
        return lax.broadcasted_iota(jnp.int32, shape, 0), lax.broadcasted_iota(jnp.int32, shape, 1)

    def side_by_side(values, axis):
        return values[0] if len(values) == 1 else jnp.concatenate(values, axis)

    places = []
    for j, g in enumerate(g_in):
        slot = lax.rem(me + j, cores)
        a, b = pos_ref[slot, 0] - m, pos_ref[slot, 1] - m
        row = pl.multiple_of(jnp.clip(a, 0, side - tall) // TAIL * TAIL, TAIL)
        lane = pl.multiple_of(jnp.clip(b, 0, side - broad) // LANES * LANES, LANES)
        i, w = grid2((tall, n))
        down = same(i + row, a + w)
        i, l = grid2((n, broad))
        wide = dot(g[...], same(l + lane, b + i)).astype(BF)
        places.append((row, lane, down, wide))

    strips = []
    for ph in range(n_row):
        start = pl.multiple_of(is_after("row", plan.rows[ph]) * (side - m), 32)
        w, l = grid2((n, side))
        spreads = []
        for z in z_in[ph]:
            b = decode(z[grads * m :, :])
            spreads.append(same(l + m, jnp.concatenate([b] * (side // n), 1) + w))
        spread = side_by_side(spreads, 0)
        strips.append((start, spread))

    across = []
    for c in range(n_col):
        after = is_after("col", plan.cols[c])
        offset = after * (edge - m)
        lane = pl.multiple_of(after * (side - edge), LANES)
        pieces = []
        downs = []
        for j, x in enumerate(x_in[c]):
            a = decode(x[n:, :LANES])[:, :n]
            i, w = grid2((side, n))
            downs.append(same(i + m, a + w))
            pieces.append([x[:n, :]] + [d_in[ph * n_col + c][j][...] for ph in range(n_row)])
        across.append((offset, lane, side_by_side(downs, 1), [jnp.concatenate(p, 0) for p in pieces]))

    per = 3
    copies = []
    for s in range(grads // per):
        acc_ref[...] = jnp.zeros_like(acc_ref)
        for k in range(per):
            p = per * s + k
            for row, lane, down, wide in places:
                acc_ref[k, pl.ds(row, tall), pl.ds(lane, broad)] += dot(down, wide[p * n : (p + 1) * n, :])
            for ph, (start, spread) in enumerate(strips):
                both = side_by_side([z[p * m : (p + 1) * m, :] for z in z_in[ph]], 1)
                acc_ref[k, pl.ds(start, m), :] += dot(both, spread)
            for offset, lane, down, pieces in across:
                low = p * m // LANES * LANES
                high = min(-(-(p * m + m) // LANES) * LANES, grads * m)
                first = p * m - low
                i, l = grid2((high - low, edge))
                pick = jnp.where((i >= first) & (i < first + m) & (i - first + offset == l), 1.0, 0.0).astype(BF)
                placed = [dot(q[:, low:high], pick) for q in pieces]
                acc_ref[k, :, pl.ds(lane, edge)] += dot(down, side_by_side([q[:n].astype(BF) for q in placed], 0))
                for ph, (start, _) in enumerate(strips):
                    rows = slice(n + ph * m, n + (ph + 1) * m)
                    acc_ref[k, pl.ds(start, m), pl.ds(lane, edge)] += sum(q[rows] for q in placed)
        inverse = 1.0 / (acc_ref[per - 1] + REGULAR)
        for k in range(2):
            out_ref[2 * s + k] = obj_ref[2 * s + k].astype(F32) - acc_ref[k] * inverse
        copy = pltpu.make_async_copy(out_ref.at[pl.ds(2 * s, 2)], out_hbm.at[pl.ds(2 * s, 2)], sem.at[s])
        copy.start()
        copies.append(copy)
    for copy in copies:
        copy.wait()


class Plan:
    def __init__(self, mesh):
        self.sizes = (mesh.shape["row"], mesh.shape["col"], mesh.shape["probe"])
        self.rows = phases_of(self.sizes[0])
        self.cols = phases_of(self.sizes[1])
        self.cores = self.sizes[2]

    def swap(self, value, row_phase, col_phase):
        return lax.ppermute(value, ("row", "col", "probe"), swap_pairs(self.sizes, row_phase, col_phase))

    def others(self, value):
        n = self.cores
        return [value] + [lax.ppermute(value, "probe", [((i + j) % n, i) for i in range(n)]) for j in range(1, n)]


def dft_pack(n):
    k = np.arange(n)
    phase = 2.0 * np.pi * ((k[:, None] * k[None, :]) % n) / n
    fr, fi = np.cos(phase) / np.sqrt(n), -np.sin(phase) / np.sqrt(n)
    return fr.astype(np.float32), fi.astype(np.float32)


def chirps(n, tilt_shift):
    u = jnp.arange(n, dtype=jnp.int32)
    u = (u + n // 2) % n - n // 2
    curve = ((u * u) % (4 * n)).astype(F32) / (4 * n)
    turns = tilt_shift[:, None] * u.astype(F32)[None, :] / n
    phase = (2.0 * np.pi) * (curve[None, :] + (turns - jnp.round(turns)))
    return jnp.stack([jnp.cos(phase), jnp.sin(phase)], 1).reshape(-1, n)


def body(plan, object_tiles, probe_modes, amplitudes, positions, counts, tilt_shift):
    slices, _, side, _ = object_tiles.shape
    planes = slices * 2
    n = probe_modes.shape[2]
    m = MARGIN
    grads = slices * 3
    slot_total = amplitudes.shape[2]
    assert slot_total == plan.cores
    obj = object_tiles.reshape(planes, side, side)
    pos = positions[0, 0]
    n_row, n_col = len(plan.rows), len(plan.cols)
    combos = [(r, c) for r in plan.rows for c in plan.cols]

    def sds(shape, dtype=BF):
        return jax.ShapeDtypeStruct(shape, dtype)

    strips = pl.pallas_call(
        functools.partial(prep_kernel, plan),
        out_shape=[sds((planes * m, side))] * n_row
        + [sds((side, planes * m))] * n_col
        + [sds((m, planes * m))] * len(combos),
        in_specs=[VMEM],
        out_specs=[VMEM] * (n_row + n_col + len(combos)),
        name="strips",
    )(obj)
    links = [(r, None) for r in plan.rows] + [(None, c) for c in plan.cols] + combos
    arrived = [plan.swap(v, *link) for v, link in zip(strips, links)]

    modes = plan.others(probe_modes)
    fr, fi = dft_pack(n)

    def np_split(x):
        hi = x.astype(jnp.bfloat16)
        return hi, (x - hi.astype(np.float32)).astype(jnp.bfloat16)

    fpack = np.block([[fr, fi], [-fi, fr]])
    fcpack = np.block([[fr, -fi], [fi, fr]])
    fpacks = jnp.asarray(np.stack([*np_split(fpack), *np_split(fcpack)]))
    props = pl.pallas_call(
        table_kernel,
        out_shape=sds((8, 2 * n, 2 * n)),
        in_specs=[VMEM, VMEM],
        out_specs=VMEM,
        name="tables",
        cost_estimate=pl.CostEstimate(flops=10**9, bytes_accessed=10**6, transcendentals=0),
    )(jnp.asarray(np.stack([fr, fi])), chirps(n, tilt_shift))

    modes_total = plan.cores * probe_modes.shape[0]
    msgs = pl.pallas_call(
        functools.partial(main_kernel, plan),
        out_shape=[sds((grads * m + TAIL, n))] * n_row
        + [sds((n + TAIL, grads * m))] * n_col
        + [sds((m, grads * m))] * len(combos)
        + [sds((grads * n, n))],
        in_specs=[SMEM, SMEM] + [VMEM] * (1 + len(links) + plan.cores + 3),
        out_specs=[VMEM] * (len(links) + 1),
        scratch_shapes=[
            pltpu.VMEM((modes_total, 2, n, n), F32),
            pltpu.VMEM((modes_total, 2, n, n), F32),
            pltpu.VMEM((grads, n, n), F32),
            pltpu.VMEM((2, modes_total * n, 2 * n), BF),
            pltpu.VMEM((2, modes_total * n, 2 * n), BF),
        ],
        compiler_params=pltpu.CompilerParams(vmem_limit_bytes=24 * 2**20),
        name="waves",
    )(pos, counts, obj, *arrived, *modes, amplitudes[0, 0], fpacks, props)
    own = plan.others(msgs[-1])
    pieces = [plan.others(plan.swap(v, *link)) for v, link in zip(msgs[:-1], links)]
    flat = list(own) + [v for group in pieces for v in group]

    updated = pl.pallas_call(
        functools.partial(final_kernel, plan),
        out_shape=sds((planes, side, side), F32),
        in_specs=[SMEM] + [VMEM] * (1 + len(flat)),
        out_specs=pl.BlockSpec(memory_space=pl.ANY),
        scratch_shapes=[
            pltpu.VMEM((3, side, side), F32),
            pltpu.VMEM((planes, side, side), F32),
            pltpu.SemaphoreType.DMA((slices,)),
        ],
        compiler_params=pltpu.CompilerParams(vmem_limit_bytes=20 * 2**20),
        name="fold",
    )(pos, obj, *flat)
    return updated.reshape(object_tiles.shape)


def solution(mesh):
    plan = Plan(mesh)
    return jax.shard_map(
        functools.partial(body, plan),
        mesh=mesh,
        in_specs=(
            P("tilt", None, "row", "col"),
            P("probe", "tilt", None, None),
            P("row", "col", "tilt", None, None),
            P("row", "col", "tilt", None),
            P(("tilt", "row"), "col"),
            P("tilt"),
        ),
        out_specs=P("tilt", None, "row", "col"),
        check_vma=False,
    )
```

```python
import functools

import jax
import jax.numpy as jnp
import numpy as np
from jax import lax
from jax.experimental import pallas as pl
from jax.experimental.pallas import tpu as pltpu
from jax.sharding import PartitionSpec as P

MARGIN = 96
FLOOR = 1.0
REGULAR = 1.0
LANES = 128
TAIL = 16
GROUP = 2
BF = jnp.bfloat16
F32 = jnp.float32
VMEM = pl.BlockSpec(memory_space=pltpu.VMEM)
SMEM = pl.BlockSpec(memory_space=pltpu.SMEM)


def partner(index, phase, size):
    other = (index ^ 1) if phase == 0 else ((index + 1) ^ 1) - 1
    return other if 0 <= other < size else None


def phases_of(size):
    return [ph for ph in (0, 1) if any(partner(i, ph, size) is not None for i in range(size))]


def swap_pairs(sizes, links):
    rows, cols, cores = sizes
    pairs = []
    for r in range(rows):
        for c in range(cols):
            for k in range(cores):
                row_phase, col_phase = links[k]
                r2 = r if row_phase is None else partner(r, row_phase, rows)
                c2 = c if col_phase is None else partner(c, col_phase, cols)
                if r2 is not None and c2 is not None:
                    pairs.append(((r * cols + c) * cores + k, (r2 * cols + c2) * cores + k))
    return pairs


def is_after(axis, phase):
    index = lax.axis_index(axis)
    return jnp.where(lax.rem(index, 2) == phase, 1, 0).astype(jnp.int32)


def onehot(shape, fn):
    i = lax.broadcasted_iota(jnp.int32, shape, 0)
    j = lax.broadcasted_iota(jnp.int32, shape, 1)
    return jnp.where(fn(i, j), 1.0, 0.0).astype(BF)


def dot(a, b):
    return jnp.dot(a, b, preferred_element_type=F32)


def split(x):
    hi = x.astype(BF)
    return hi, (x - hi.astype(F32)).astype(BF)


def prep_kernel(plan, obj_ref, z_ref, *refs):
    n_col = len(plan.cols)
    x_refs, d_refs = refs[:n_col], refs[n_col : 2 * n_col]
    edge_refs, sem = refs[2 * n_col : -1], refs[-1]
    planes, side, _ = obj_ref.shape
    m = MARGIN
    part = x_refs[0].shape[0]
    edge = edge_refs[0].shape[2]
    me = lax.axis_index("probe")
    start = pl.multiple_of(is_after("row", me) * (side - m), 32)
    share = pl.multiple_of(me * part, 32)
    copies = [pltpu.make_async_copy(obj_ref.at[:, pl.ds(start, m), :], z_ref, sem.at[0])]
    lanes = []
    for c, pc in enumerate(plan.cols):
        lanes.append(pl.multiple_of(is_after("col", pc) * (side - edge), LANES))
        source = obj_ref.at[:, pl.ds(share, part), pl.ds(lanes[c], edge)]
        copies.append(pltpu.make_async_copy(source, edge_refs[c], sem.at[1 + c]))
    for copy in copies:
        copy.start()
    j = lax.broadcasted_iota(jnp.int32, (1, planes * m), 1)
    picks = []
    for c, pc in enumerate(plan.cols):
        wanted = (j // m) * edge + j % m + is_after("col", pc) * (edge - m)
        i = lax.broadcasted_iota(jnp.int32, (planes * edge, planes * m), 0)
        picks.append(jnp.where(i == wanted, 1.0, 0.0).astype(BF))
    for copy in copies:
        copy.wait()
    for c in range(n_col):
        rows = jnp.concatenate([edge_refs[c][p] for p in range(planes)], 1)
        x_refs[c][...] = dot(rows, picks[c]).astype(BF)
        rows = jnp.concatenate([z_ref[p, :, pl.ds(lanes[c], edge)] for p in range(planes)], 1)
        d_refs[c][...] = dot(rows, picks[c]).astype(BF)


def right_pack(re, im):
    return jnp.concatenate([jnp.concatenate([re, im], 1), jnp.concatenate([-im, re], 1)], 0)


def left_pack(re, im):
    return jnp.concatenate([jnp.concatenate([re, -im], 1), jnp.concatenate([im, re], 1)], 0)


def table_kernel(f_ref, h_ref, out_ref):
    n = f_ref.shape[1]
    fr, fi = f_ref[0], f_ref[1]

    def circulant(hr, hi):
        vr, vi = fr * hr + fi * hi, fr * hi - fi * hr
        a_hi, a_lo = split(left_pack(vr, vi))
        b_hi, b_lo = split(left_pack(fr, fi))
        return dot(a_hi, b_hi) + (dot(a_lo, b_hi) + dot(a_hi, b_lo)) + dot(a_lo, b_lo)

    def store(at, value):
        hi, lo = split(value)
        out_ref[2 * at] = hi
        out_ref[2 * at + 1] = lo

    for axis in (0, 1):
        table = circulant(h_ref[2 * axis : 2 * axis + 1, :], h_ref[2 * axis + 1 : 2 * axis + 2, :])
        store(2 * axis, table.T)
        store(2 * axis + 1, table)


def main_kernel(plan, *refs):
    refs = list(refs)
    pos_ref, cnt_ref, obj_ref = refs[:3]
    refs = refs[3:]
    n_row, n_col, cores = len(plan.rows), len(plan.cols), plan.cores

    def take(k):
        nonlocal refs
        head, refs = refs[:k], refs[k:]
        return head

    z_in = take(cores)
    x_in = [take(cores) for _ in range(n_col)]
    d_in = [take(cores) for _ in range(n_col)]
    q_refs = take(cores)
    amp_ref, fpack_ref, prop_ref = take(3)
    z_out = take(n_row)
    x_out = take(n_col)
    d_out = take(n_row * n_col)
    g_out, wave_ref, far_ref, gsum_ref, hi_ref, lo_ref = refs

    planes, side, _ = obj_ref.shape
    n = amp_ref.shape[1]
    m = MARGIN
    slot = lax.axis_index("probe")
    a, b = pos_ref[slot, 0], pos_ref[slot, 1]
    live = slot < cnt_ref[0, 0]

    row0 = [is_after("row", ph) * (side + m) for ph in plan.rows]
    col0 = [is_after("col", ph) * (side + m) for ph in plan.cols]

    tall, broad = n + TAIL, min(n + LANES, side)
    row = pl.multiple_of(jnp.clip(a - m, 0, side - tall) // TAIL * TAIL, TAIL)
    lane = pl.multiple_of(jnp.clip(b - m, 0, side - broad) // LANES * LANES, LANES)
    r_own = onehot((n, tall), lambda i, j: j + row + m == a + i)
    c_own = onehot((broad, n), lambda i, j: i + lane + m == b + j)
    part = x_in[0][0].shape[0] if n_col else side
    holders = [lax.rem(slot + j, cores) for j in range(cores)]
    r_strip = [onehot((n, m), lambda i, j, o=is_after("row", k) * (side + m): j + o == a + i) for k in holders]
    r_part = [onehot((n, part), lambda i, j, o=k * part + m: j + o == a + i) for k in holders]

    packed = []
    for c in range(n_col):
        value = sum(dot(r_part[k], x_in[c][k][...]) + dot(r_strip[k], d_in[c][k][...]) for k in range(cores))
        packed.append(value.astype(BF))

    def lanes_of(p, total):
        low = p * m // LANES * LANES
        return low, min(-(-(p * m + m) // LANES) * LANES, total), p * m - low

    window = []
    for p in range(planes):
        cut = dot(r_own, obj_ref[p, pl.ds(row, tall), pl.ds(lane, broad)])
        for k in range(cores):
            cut += dot(r_strip[k], z_in[k][p, :, pl.ds(lane, broad)])
        value = dot(cut.astype(BF), c_own)
        low, high, first = lanes_of(p, planes * m)
        for c in range(n_col):
            pick = onehot(
                (high - low, n),
                lambda i, j, o=col0[c] - first: (i >= first) & (i < first + m) & (i + o == b + j),
            )
            value += dot(packed[c][:, low:high], pick)
        window.append(value)
    p1r, p1i, p2r, p2i = window

    p2r, p2i = p2r.T, p2i.T

    dft = (fpack_ref[0], fpack_ref[1])
    inv = (fpack_ref[2], fpack_ref[3])
    fwd_rows, adj_rows, fwd_cols, adj_cols = ((prop_ref[2 * k], prop_ref[2 * k + 1]) for k in range(4))

    local = q_refs[0].shape[0]
    modes = local * plan.cores
    group = min(GROUP, modes)

    def probe(mode):
        q = q_refs[mode // local]
        return q[mode % local, 0].astype(F32), q[mode % local, 1].astype(F32)

    def put(side, mode, re, im):
        rows = slice(mode * n, (mode + 1) * n)
        for part, value in enumerate((re, im)):
            hi, lo = split(value)
            lanes = slice(part * n, (part + 1) * n)
            hi_ref[side, rows, lanes] = hi
            lo_ref[side, rows, lanes] = lo

    queue = []

    def product(side, table, finish):
        t_hi, t_lo = table
        for first in range(0, modes, group):
            rows = slice(first * n, (first + group) * n)
            hi, lo = hi_ref[side, rows, :], lo_ref[side, rows, :]
            y = dot(hi, t_hi) + dot(lo, t_hi) + dot(hi, t_lo)
            parts = [(y[i * n : (i + 1) * n, :n], y[i * n : (i + 1) * n, n:]) for i in range(group)]
            queue.append(functools.partial(finish, first, parts))
            if len(queue) > 1:
                queue.pop(0)()

    def drain():
        while queue:
            queue.pop(0)()

    def turned(side):
        def finish(first, parts):
            for i, (re, im) in enumerate(parts):
                put(side, first + i, re.T, im.T)

        return finish

    for mode in range(modes):
        qr, qi = probe(mode)
        put(0, mode, qr * p1r - qi * p1i, qr * p1i + qi * p1r)

    def at_slice_2(first, parts):
        for i, (wr, wi) in enumerate(parts):
            wave_ref[first + i, 0] = wr
            wave_ref[first + i, 1] = wi
            put(0, first + i, wr * p2r - wi * p2i, wr * p2i + wi * p2r)

    def at_detector(first, parts):
        total = sum(fr * fr + fi * fi for fr, fi in parts)
        gsum_ref[0] = total if first == 0 else gsum_ref[0] + total
        for i, (fr, fi) in enumerate(parts):
            far_ref[first + i, 0] = fr
            far_ref[first + i, 1] = fi

    product(0, fwd_cols, turned(1))
    product(1, fwd_rows, at_slice_2)
    product(0, dft, turned(1))
    product(1, dft, at_detector)
    drain()

    factor = 1.0 - amp_ref[slot].astype(F32) / jnp.maximum(jnp.sqrt(gsum_ref[0]), FLOOR)
    for mode in range(modes):
        put(0, mode, far_ref[mode, 0] * factor, far_ref[mode, 1] * factor)

    def back_at_slice_2(first, parts):
        sums = [0.0, 0.0, 0.0]
        for i, (br, bi) in enumerate(parts):
            wr, wi = wave_ref[first + i, 0], wave_ref[first + i, 1]
            sums[0] += wr * br + wi * bi
            sums[1] += wr * bi - wi * br
            sums[2] += wr * wr + wi * wi
            put(0, first + i, p2r * br + p2i * bi, p2r * bi - p2i * br)
        for k, value in enumerate(sums):
            gsum_ref[3 + k] = value if first == 0 else gsum_ref[3 + k] + value

    def back_at_slice_1(first, parts):
        sums = [0.0, 0.0, 0.0]
        for i, (er, ei) in enumerate(parts):
            qr, qi = probe(first + i)
            sums[0] += qr * er + qi * ei
            sums[1] += qr * ei - qi * er
            sums[2] += qr * qr + qi * qi
        for k, value in enumerate(sums):
            gsum_ref[k] = value if first == 0 else gsum_ref[k] + value

    product(0, inv, turned(1))
    product(1, inv, back_at_slice_2)
    product(0, adj_rows, turned(1))
    product(1, adj_cols, back_at_slice_1)
    drain()
    for k in range(3, 6):
        gsum_ref[k] = gsum_ref[k].T

    grads = gsum_ref.shape[0]
    for p in range(grads):
        g_out[p * n : (p + 1) * n, :] = jnp.where(live, gsum_ref[p], 0.0).astype(BF)

    def digits(shape, value):
        i = lax.broadcasted_iota(jnp.int32, shape, 0)
        high = lax.shift_right_logical(value, 4)
        low = value & 15
        return jnp.where(i == 0, high, jnp.where(i == 1, low, 0)).astype(F32).astype(BF)

    r_out = [onehot((m, n), lambda i, j, o=o: i + o == a + j) for o in row0]
    for z, r in zip(z_out, r_out):
        for p in range(grads):
            z[p * m : (p + 1) * m, :] = dot(r, g_out[p * n : (p + 1) * n, :]).astype(BF)
        z[grads * m :, :] = digits((TAIL, n), b)
    for c, x in enumerate(x_out):
        value = {}
        for p in range(grads):
            low, high, first = lanes_of(p, grads * m)
            pick = onehot(
                (n, high - low),
                lambda i, j, o=col0[c] - first: (j >= first) & (j < first + m) & (j + o == b + i),
            )
            term = dot(g_out[p * n : (p + 1) * n, :], pick)
            for at in range(low, high, LANES):
                here = term[:, at - low : min(at + LANES, high) - low]
                value[at] = here if at not in value else value[at] + here
        x[:n, :] = jnp.concatenate([value[at] for at in sorted(value)], 1).astype(BF)
        x[n:, :] = digits((TAIL, grads * m), a)
        for ph, r in enumerate(r_out):
            d_out[ph * n_col + c][...] = dot(r, x[:n, :]).astype(BF)


def final_kernel(plan, *refs):
    refs = list(refs)
    pos_ref, obj_ref = refs[:2]
    refs = refs[2:]
    n_row, n_col, cores = len(plan.rows), len(plan.cols), plan.cores

    def take(k):
        nonlocal refs
        head, refs = refs[:k], refs[k:]
        return head

    g_in = take(cores)
    z_in = [take(cores) for _ in range(n_row)]
    x_in = [take(cores) for _ in range(n_col)]
    d_in = [take(cores) for _ in range(n_row * n_col)]
    out_hbm, acc_ref, out_ref, sem = refs

    planes, side, _ = obj_ref.shape
    n = g_in[0].shape[1]
    m = MARGIN
    grads = g_in[0].shape[0] // n
    me = lax.axis_index("probe")
    edge = -(-m // LANES) * LANES
    tall, broad = n + TAIL, min(n + LANES, side)

    def decode(value):
        return (value[0:1, :].astype(F32) * 16.0 + value[1:2, :].astype(F32)).astype(jnp.int32)

    def same(left, right):
        return jnp.where(left == right, 1.0, 0.0).astype(BF)

    def grid2(shape):
        return lax.broadcasted_iota(jnp.int32, shape, 0), lax.broadcasted_iota(jnp.int32, shape, 1)

    def side_by_side(values, axis):
        return values[0] if len(values) == 1 else jnp.concatenate(values, axis)

    places = []
    for j, g in enumerate(g_in):
        slot = lax.rem(me + j, cores)
        a, b = pos_ref[slot, 0] - m, pos_ref[slot, 1] - m
        row = pl.multiple_of(jnp.clip(a, 0, side - tall) // TAIL * TAIL, TAIL)
        lane = pl.multiple_of(jnp.clip(b, 0, side - broad) // LANES * LANES, LANES)
        i, w = grid2((tall, n))
        down = same(i + row, a + w)
        i, l = grid2((n, broad))
        wide = dot(g[...], same(l + lane, b + i)).astype(BF)
        places.append((row, lane, down, wide))

    strips = []
    for ph in range(n_row):
        start = pl.multiple_of(is_after("row", plan.rows[ph]) * (side - m), 32)
        w, l = grid2((n, side))
        spreads = []
        for z in z_in[ph]:
            b = decode(z[grads * m :, :])
            spreads.append(same(l + m, jnp.concatenate([b] * (side // n), 1) + w))
        spread = side_by_side(spreads, 0)
        strips.append((start, spread))

    across = []
    for c in range(n_col):
        after = is_after("col", plan.cols[c])
        offset = after * (edge - m)
        lane = pl.multiple_of(after * (side - edge), LANES)
        pieces = []
        downs = []
        for j, x in enumerate(x_in[c]):
            a = decode(x[n:, :LANES])[:, :n]
            i, w = grid2((side, n))
            downs.append(same(i + m, a + w))
            pieces.append([x[:n, :]] + [d_in[ph * n_col + c][j][...] for ph in range(n_row)])
        across.append((offset, lane, side_by_side(downs, 1), [jnp.concatenate(p, 0) for p in pieces]))

    per = 3
    copies = []
    for s in range(grads // per):
        acc_ref[...] = jnp.zeros_like(acc_ref)
        for k in range(per):
            p = per * s + k
            for row, lane, down, wide in places:
                acc_ref[k, pl.ds(row, tall), pl.ds(lane, broad)] += dot(down, wide[p * n : (p + 1) * n, :])
            for ph, (start, spread) in enumerate(strips):
                both = side_by_side([z[p * m : (p + 1) * m, :] for z in z_in[ph]], 1)
                acc_ref[k, pl.ds(start, m), :] += dot(both, spread)
            for offset, lane, down, pieces in across:
                low = p * m // LANES * LANES
                high = min(-(-(p * m + m) // LANES) * LANES, grads * m)
                first = p * m - low
                i, l = grid2((high - low, edge))
                pick = jnp.where((i >= first) & (i < first + m) & (i - first + offset == l), 1.0, 0.0).astype(BF)
                placed = [dot(q[:, low:high], pick) for q in pieces]
                acc_ref[k, :, pl.ds(lane, edge)] += dot(down, side_by_side([q[:n].astype(BF) for q in placed], 0))
                for ph, (start, _) in enumerate(strips):
                    rows = slice(n + ph * m, n + (ph + 1) * m)
                    acc_ref[k, pl.ds(start, m), pl.ds(lane, edge)] += sum(q[rows] for q in placed)
        inverse = 1.0 / (acc_ref[per - 1] + REGULAR)
        for k in range(2):
            out_ref[2 * s + k] = obj_ref[2 * s + k].astype(F32) - acc_ref[k] * inverse
        copy = pltpu.make_async_copy(out_ref.at[pl.ds(2 * s, 2)], out_hbm.at[pl.ds(2 * s, 2)], sem.at[s])
        copy.start()
        copies.append(copy)
    for copy in copies:
        copy.wait()


class Plan:
    def __init__(self, mesh):
        self.sizes = (mesh.shape["row"], mesh.shape["col"], mesh.shape["probe"])
        self.rows = phases_of(self.sizes[0])
        self.cols = phases_of(self.sizes[1])
        self.cores = self.sizes[2]

    def swap(self, value, links):
        return lax.ppermute(value, ("row", "col", "probe"), swap_pairs(self.sizes, links))

    def others(self, value):
        n = self.cores
        return [value] + [lax.ppermute(value, "probe", [((i + j) % n, i) for i in range(n)]) for j in range(1, n)]


def dft_pack(n):
    k = np.arange(n)
    phase = 2.0 * np.pi * ((k[:, None] * k[None, :]) % n) / n
    fr, fi = np.cos(phase) / np.sqrt(n), -np.sin(phase) / np.sqrt(n)
    return fr.astype(np.float32), fi.astype(np.float32)


def chirps(n, tilt_shift):
    u = jnp.arange(n, dtype=jnp.int32)
    u = (u + n // 2) % n - n // 2
    curve = ((u * u) % (4 * n)).astype(F32) / (4 * n)
    turns = tilt_shift[:, None] * u.astype(F32)[None, :] / n
    phase = (2.0 * np.pi) * (curve[None, :] + (turns - jnp.round(turns)))
    return jnp.stack([jnp.cos(phase), jnp.sin(phase)], 1).reshape(-1, n)


def body(plan, object_tiles, probe_modes, amplitudes, positions, counts, tilt_shift):
    slices, _, side, _ = object_tiles.shape
    planes = slices * 2
    n = probe_modes.shape[2]
    m = MARGIN
    grads = slices * 3
    slot_total = amplitudes.shape[2]
    assert slot_total == plan.cores
    obj = object_tiles.reshape(planes, side, side)
    pos = positions[0, 0]
    n_row, n_col = len(plan.rows), len(plan.cols)
    combos = [(r, c) for r in plan.rows for c in plan.cols]

    def sds(shape, dtype=BF):
        return jax.ShapeDtypeStruct(shape, dtype)

    cores = plan.cores
    assert cores >= n_row and side % cores == 0
    edge = -(-m // LANES) * LANES
    strips = pl.pallas_call(
        functools.partial(prep_kernel, plan),
        out_shape=[sds((planes, m, side))] + [sds((side // cores, planes * m))] * n_col + [sds((m, planes * m))] * n_col,
        in_specs=[pl.BlockSpec(memory_space=pltpu.HBM)],
        out_specs=[VMEM] * (1 + 2 * n_col),
        scratch_shapes=[pltpu.VMEM((planes, side // cores, edge), BF)] * n_col + [pltpu.SemaphoreType.DMA((1 + n_col,))],
        compiler_params=pltpu.CompilerParams(vmem_limit_bytes=8 * 2**20),
        name="strips",
    )(obj)
    every = range(cores)
    by_core = [[(k, None) for k in every]]
    by_core += [[(None, c) for _ in every] for c in plan.cols]
    by_core += [[(k, c) for k in every] for c in plan.cols]
    names = ["z"] + ["x"] * n_col + ["d"] * n_col
    arrived = []
    for name, v, link in zip(names, strips, by_core):
        with jax.named_scope("halo_" + name):
            v = plan.swap(v, link)
        arrived.append(v)
    halos = []
    for name, v in zip(names, arrived):
        with jax.named_scope("core_" + name):
            halos += plan.others(v)
    links = [(r, None) for r in plan.rows] + [(None, c) for c in plan.cols] + combos

    with jax.named_scope("core_q"):
        modes = plan.others(probe_modes)
    fr, fi = dft_pack(n)

    def np_split(x):
        hi = x.astype(jnp.bfloat16)
        return hi, (x - hi.astype(np.float32)).astype(jnp.bfloat16)

    fpack = np.block([[fr, fi], [-fi, fr]])
    fcpack = np.block([[fr, -fi], [fi, fr]])
    fpacks = jnp.asarray(np.stack([*np_split(fpack), *np_split(fcpack)]))
    props = pl.pallas_call(
        table_kernel,
        out_shape=sds((8, 2 * n, 2 * n)),
        in_specs=[VMEM, VMEM],
        out_specs=VMEM,
        compiler_params=pltpu.CompilerParams(vmem_limit_bytes=8 * 2**20),
        name="tables",
        cost_estimate=pl.CostEstimate(flops=10**9, bytes_accessed=10**6, transcendentals=0),
    )(jnp.asarray(np.stack([fr, fi])), chirps(n, tilt_shift))

    modes_total = plan.cores * probe_modes.shape[0]
    msgs = pl.pallas_call(
        functools.partial(main_kernel, plan),
        out_shape=[sds((grads * m + TAIL, n))] * n_row
        + [sds((n + TAIL, grads * m))] * n_col
        + [sds((m, grads * m))] * len(combos)
        + [sds((grads * n, n))],
        in_specs=[SMEM, SMEM] + [VMEM] * (1 + len(halos) + plan.cores + 3),
        out_specs=[VMEM] * (len(links) + 1),
        scratch_shapes=[
            pltpu.VMEM((modes_total, 2, n, n), F32),
            pltpu.VMEM((modes_total, 2, n, n), F32),
            pltpu.VMEM((grads, n, n), F32),
            pltpu.VMEM((2, modes_total * n, 2 * n), BF),
            pltpu.VMEM((2, modes_total * n, 2 * n), BF),
        ],
        compiler_params=pltpu.CompilerParams(vmem_limit_bytes=24 * 2**20),
        name="waves",
    )(pos, counts, obj, *halos, *modes, amplitudes[0, 0], fpacks, props)
    own = plan.others(msgs[-1])
    pieces = [plan.others(plan.swap(v, [link] * cores)) for v, link in zip(msgs[:-1], links)]
    flat = list(own) + [v for group in pieces for v in group]

    updated = pl.pallas_call(
        functools.partial(final_kernel, plan),
        out_shape=sds((planes, side, side), F32),
        in_specs=[SMEM] + [VMEM] * (1 + len(flat)),
        out_specs=pl.BlockSpec(memory_space=pl.ANY),
        scratch_shapes=[
            pltpu.VMEM((3, side, side), F32),
            pltpu.VMEM((planes, side, side), F32),
            pltpu.SemaphoreType.DMA((slices,)),
        ],
        compiler_params=pltpu.CompilerParams(vmem_limit_bytes=20 * 2**20),
        name="fold",
    )(pos, obj, *flat)
    return updated.reshape(object_tiles.shape)


def solution(mesh):
    plan = Plan(mesh)
    return jax.shard_map(
        functools.partial(body, plan),
        mesh=mesh,
        in_specs=(
            P("tilt", None, "row", "col"),
            P("probe", "tilt", None, None),
            P("row", "col", "tilt", None, None),
            P("row", "col", "tilt", None),
            P(("tilt", "row"), "col"),
            P("tilt"),
        ),
        out_specs=P("tilt", None, "row", "col"),
        check_vma=False,
    )
```
